32 devices in a mesh: dp: 2 (over y), expert: 4 (over x, core), tensor: 4 (over z).
Axes of the slice: x: 2, y: 2, z: 4, core: 2. Of those that a mesh axis runs over, the one named last changes fastest.
Arguments:
- conv_out: bfloat16 [16, 2, 8192], P('dp', None, ('expert', 'tensor')), may hold values from -6 to 6
- gate_in: bfloat16 [16, 2, 8192], P('dp', None, ('expert', 'tensor')), may hold values from -6 to 6
- dt_low: bfloat16 [16, 2, 512], P('dp'), may hold values from -6 to 6
- state_proj: float32 [16, 2, 2, 16], P('dp'), may hold values from -6 to 6
- dt_weight: bfloat16 [512, 8192], P(None, ('expert', 'tensor')), may hold values from -0.25 to 0.25
- dt_bias: float32 [8192], P(('expert', 'tensor')), may hold values from -3 to 0.5
- decay_rate: float32 [16, 8192], P(None, ('expert', 'tensor')), may hold values from 0.05 to 16
- skip_gain: float32 [8192], P(('expert', 'tensor')), may hold values from 0.2 to 1.5
- states: float32 [32, 16, 8192], P('dp', None, ('expert', 'tensor')), may hold values from -6 to 6
- slot_ids: int32 [16], P('dp'), may hold values from 0 to 15, as said below
- out_proj: bfloat16 [8192, 4096], P(('expert', 'tensor')), may hold values from -0.09375 to 0.09375
- stream: bfloat16 [16, 2, 4096], P(('dp', 'expert')), may hold values from -6 to 6
- norm_gain: float32 [4096], replicated, may hold values from 0.5 to 1.5
- router: bfloat16 [4096, 4], replicated, may hold values from -0.0234375 to 0.0234375
- routes: int32 [16, 2, 2], P(('dp', 'expert')), may hold values from 0 to 3, as said below
- gate_w: bfloat16 [4, 4096, 12288], P('expert', None, ('dp', 'tensor')), may hold values from -0.09375 to 0.09375
- up_w: bfloat16 [4, 4096, 12288], P('expert', None, ('dp', 'tensor')), may hold values from -0.09375 to 0.09375
- down_w: bfloat16 [4, 12288, 4096], P('expert', ('dp', 'tensor')), may hold values from -0.3125 to 0.3125
Outputs:
- new_states: float32 [32, 16, 8192], P('dp', None, ('expert', 'tensor'))
- mixed: bfloat16 [16, 2, 4096], P(('dp', 'expert'), None, 'tensor')
The draws below stay inside these ranges and needn't reach their ends.
Inputs may be any that keep to these rules, and one draw needn't show every extreme that they name: `slot_ids`: within the rows of one dp index (each 8 rows in order) the slots differ. `routes`: the experts of one token differ; among the tokens of one device, each 2 rows with all 2 steps, no expert is named more than 4 times; in every draw some expert is named exactly 4 times by the tokens of every device.
All inputs are finite; a program needn't handle non-finite values.
Results may differ from the reference program's by a relative error of at most 0.011.
Values may be sent and summed in bfloat16 or wider, within the bound.
A program may use at most 128 MiB of HBM per device.

```python
import math
import jax
import jax.numpy as jnp
from jax import lax

D = 4096
DI = 8192
N = 16
R = 512
FF = 12288
TOP = 2
STEPS = 2
ROW_DEV = 2
SLOT_DEV = 16
EXPERTS = 4
ROWS = 16
GROUP_ROWS = 8
SLOTS = 32
CAPACITY = 4


def draw_slot_ids(key, part):
    group_count = ROWS // GROUP_ROWS
    group_keys = jax.random.split(jax.random.fold_in(key, 7), group_count)
    orders = jax.vmap(lambda group_key: jax.random.permutation(group_key, SLOT_DEV))(group_keys)
    return orders[:, :GROUP_ROWS].reshape(-1).astype(jnp.int32)


def draw_routes(key, part):
    block_size = ROW_DEV * STEPS
    block_count = ROWS // ROW_DEV
    base_key = jax.random.fold_in(key, 11)
    order_key, light_key, flip_key, shuffle_key = jax.random.split(base_key, 4)
    order_keys = jax.random.split(order_key, block_count)
    expert_order = jax.vmap(lambda order_one: jax.random.permutation(order_one, EXPERTS))(order_keys).astype(jnp.int32)
    token_index = jnp.arange(block_size, dtype=jnp.int32)
    has_first = token_index < CAPACITY
    has_second = token_index >= block_size - CAPACITY
    single = jnp.logical_xor(has_first, has_second).astype(jnp.int32)
    single_rank = jnp.cumsum(single) - single
    light_kinds = EXPERTS - 2
    offsets = jax.random.randint(light_key, (block_count, 1), 0, light_kinds, dtype=jnp.int32)
    light_pick = ((single_rank[None, :] + offsets) % light_kinds + 2).astype(jnp.int32)
    light_expert = jnp.take_along_axis(expert_order, light_pick, axis=1)
    first_pick = jnp.where(has_first[None, :], expert_order[:, 0:1], expert_order[:, 1:2])
    both_heavy = jnp.broadcast_to((has_first & has_second)[None, :], (block_count, block_size))
    second_pick = jnp.where(both_heavy, expert_order[:, 1:2], light_expert)
    flip_bits = jax.random.randint(flip_key, (block_count, block_size), 0, 2, dtype=jnp.int32)
    lead_pick = jnp.where(flip_bits == 1, second_pick, first_pick)
    trail_pick = jnp.where(flip_bits == 1, first_pick, second_pick)
    chosen_pairs = jnp.stack([lead_pick, trail_pick], axis=-1)
    shuffle_keys = jax.random.split(shuffle_key, block_count)
    orders = jax.vmap(lambda shuffle_one: jax.random.permutation(shuffle_one, block_size))(shuffle_keys).astype(jnp.int32)
    chosen_pairs = jnp.take_along_axis(chosen_pairs, orders[:, :, None], axis=1)
    return chosen_pairs.reshape(ROWS, STEPS, TOP).astype(jnp.int32)


def spiked(entries, stream_key, source, target, shards_of, factor):
    owner, partner = [(jnp.arange(entries.shape[position]) // (entries.shape[position] // shards_of)).reshape([-1 if axis == position else 1 for axis in range(entries.ndim)]) for position in (source, target)]
    chosen = jax.random.permutation(stream_key, shards_of)[partner]
    strong = (owner == chosen) | (owner == (partner + shards_of // 2) % shards_of)
    return jnp.where(strong, factor * entries, entries)


def levels(rng, extent, shards, smallest, high):
    loudness = 1.0
    for dim, parts in shards:
        steps = jax.random.uniform(jax.random.fold_in(jax.random.fold_in(rng, 6), dim), (parts,), jnp.float32, smallest / len(shards), high / len(shards))
        loudness = loudness * jnp.repeat(jnp.exp(steps), extent[dim] // parts).reshape((-1,) + (1,) * (len(extent) - 1 - dim))
    return loudness


def scatter_about(rng, shape, scale, reach, shards=(), held_as=jnp.bfloat16):
    entries = scale * jax.random.normal(rng, shape, jnp.float32)
    if shards:
        entries = entries * levels(rng, shape, shards, -0.22, 0.18)
    return jnp.clip(entries, -reach, reach).astype(held_as)


def gaussian_with(own_key, extent, deviation, bound, pieces, heavy, kind=jnp.bfloat16):
    array = deviation * jax.random.normal(own_key, extent, jnp.float32)
    if pieces:
        array = array * levels(own_key, extent, pieces, -0.22, 0.18)
    return jnp.clip(spiked(array, jax.random.fold_in(own_key, 3), *heavy), -bound, bound).astype(kind)


def setup_inputs(seed: int = 0) -> dict:
    key_list = jax.random.split(jax.random.key(seed), 19)
    conv_out = scatter_about(key_list[0], (ROWS, STEPS, DI), 1.0, 6.0, ((0, 2), (2, 16)))
    gate_in = scatter_about(key_list[1], (ROWS, STEPS, DI), 1.0, 6.0, ((0, 2), (2, 16)))
    dt_low = scatter_about(key_list[2], (ROWS, STEPS, R), 1.0, 6.0, ((0, 2),))
    state_proj = scatter_about(key_list[3], (ROWS, STEPS, 2, N), 1.0, 6.0, ((0, 2),), jnp.float32)
    dt_weight = scatter_about(key_list[4], (R, DI), R ** -0.5, 0.25, ((1, 16),))
    dt_bias = jnp.clip(-3.0 + 3.5 * jax.random.uniform(key_list[5], (DI,), jnp.float32) ** levels(key_list[5], (DI,), ((0, 16),), -0.2, 0.2), -3.0, 0.5)
    decay_rate = jnp.clip(jnp.exp(math.log(16.0) - 5.768321 * jax.random.uniform(key_list[6], (N, DI), jnp.float32) ** levels(key_list[6], (N, DI), ((1, 16),), -0.2, 0.2)), 0.05, 16.0)
    skip_gain = jnp.clip(0.2 + 1.3 * jax.random.uniform(key_list[7], (DI,), jnp.float32) ** levels(key_list[7], (DI,), ((0, 16),), -0.2, 0.2), 0.2, 1.5)
    states = scatter_about(key_list[8], (SLOTS, N, DI), 1.0, 6.0, ((0, 2), (2, 16)), jnp.float32)
    slot_ids = draw_slot_ids(jax.random.fold_in(key_list[18], 71), 0)
    out_proj = gaussian_with(key_list[10], (DI, D), DI ** -0.5, 0.09375, ((0, 16),), (0, 1, 16, 2.0))
    stream = scatter_about(key_list[11], (ROWS, STEPS, D), 1.0, 6.0, ((0, 8),))
    norm_gain = jnp.clip(1.0 + 0.1 * jax.random.normal(key_list[12], (D,), jnp.float32), 0.5, 1.5)
    router = scatter_about(key_list[13], (D, EXPERTS), (D * 16) ** -0.5, 0.0234375)
    routes = draw_routes(jax.random.fold_in(key_list[18], 71), 0)
    gate_w = scatter_about(key_list[15], (EXPERTS, D, FF), D ** -0.5, 0.09375, ((0, 4), (2, 8)))
    up_w = scatter_about(key_list[16], (EXPERTS, D, FF), D ** -0.5, 0.09375, ((0, 4), (2, 8)))
    down_w = gaussian_with(key_list[17], (EXPERTS, FF, D), (FF // 16) ** -0.5, 0.3125, ((0, 4), (1, 8)), (1, 2, 8, 2.0))
    return dict(conv_out=conv_out, gate_in=gate_in, dt_low=dt_low, state_proj=state_proj, dt_weight=dt_weight, dt_bias=dt_bias, decay_rate=decay_rate, skip_gain=skip_gain, states=states, slot_ids=slot_ids, out_proj=out_proj, stream=stream, norm_gain=norm_gain, router=router, routes=routes, gate_w=gate_w, up_w=up_w, down_w=down_w)


def reference(conv_out, gate_in, dt_low, state_proj, dt_weight, dt_bias, decay_rate, skip_gain, states, slot_ids, out_proj, stream, norm_gain, router, routes, gate_w, up_w, down_w):
    row_count = conv_out.shape[0]
    slot_global = slot_ids + jnp.arange(row_count, dtype=jnp.int32) // GROUP_ROWS * SLOT_DEV
    slot_global = slot_global.astype(jnp.int32)
    carried = states[slot_global]
    low_flat = dt_low.reshape(row_count * STEPS, R)
    step_size = jnp.dot(low_flat, dt_weight, preferred_element_type=jnp.float32).reshape(row_count, STEPS, DI)
    step_size = jax.nn.softplus(step_size + dt_bias)
    inputs = conv_out.astype(jnp.float32)
    gates = gate_in.astype(jnp.float32)
    outputs = []
    for step_no in range(STEPS):
        decay = jnp.exp(-step_size[:, step_no, None, :] * decay_rate[None, :, :])
        driven = (step_size[:, step_no] * inputs[:, step_no])[:, None, :]
        carried = decay * carried + driven * state_proj[:, step_no, 0, :, None]
        read_out = lax.optimization_barrier(jnp.sum(state_proj[:, step_no, 1, :, None] * carried, axis=1)) + skip_gain * inputs[:, step_no]
        outputs.append(read_out * jax.nn.silu(gates[:, step_no]))
    mixer_y = jnp.stack(outputs, axis=1).astype(jnp.bfloat16)
    new_states = states.at[slot_global].set(carried)
    mixer_out = jnp.dot(mixer_y.reshape(row_count * STEPS, DI), out_proj, preferred_element_type=jnp.float32)
    residual = stream.reshape(row_count * STEPS, D).astype(jnp.float32) + mixer_out
    scale = jax.lax.rsqrt(lax.optimization_barrier(jnp.mean(residual * residual, axis=1, keepdims=True)) + 1e-05)
    normed = (residual * scale * norm_gain).astype(jnp.bfloat16)
    logits = jnp.dot(normed, router, preferred_element_type=jnp.float32)
    expert_ids = routes.reshape(row_count * STEPS, TOP)
    picked = jnp.take_along_axis(logits, expert_ids, axis=1)
    first_weight = jax.nn.sigmoid(picked[:, 0] - picked[:, 1])
    weights = jnp.stack([first_weight, 1.0 - first_weight], axis=1)
    combined = jnp.zeros((row_count * STEPS, D), jnp.float32)
    for expert_no in range(EXPERTS):
        gate_part = jnp.dot(normed, gate_w[expert_no], preferred_element_type=jnp.float32)
        up_part = jnp.dot(normed, up_w[expert_no], preferred_element_type=jnp.float32)
        hidden = (jax.nn.silu(gate_part) * up_part).astype(jnp.bfloat16)
        expert_out = jnp.dot(hidden, down_w[expert_no], preferred_element_type=jnp.float32)
        coeff = lax.optimization_barrier(jnp.sum(weights * (expert_ids == expert_no).astype(jnp.float32), axis=1))
        combined = combined + coeff[:, None] * expert_out
    mixed = (residual + combined).astype(jnp.bfloat16).reshape(row_count, STEPS, D)
    return (new_states, mixed)
```

```python
import functools

import jax
import jax.numpy as jnp
from jax import lax
from jax.experimental import pallas as pl
from jax.experimental.pallas import tpu as pltpu
from jax.sharding import PartitionSpec as P

MESH = pl.DeviceIdType.MESH
UNROLL_LIMIT = 64
F32 = jnp.float32
BF16 = jnp.bfloat16


def tile_of(extent):
    return 512 if extent % 512 == 0 else extent


def silu(v):
    return v / (1.0 + jnp.exp(-v))


def each(count, unroll, body):
    if unroll:
        for j in range(count):
            body(j)
    else:

        def step(j, carry):
            body(j)
            return carry

        lax.fori_loop(0, count, step, 0)


def kernel(
    sizes,
    conv_ref,
    gate_in_ref,
    low_ref,
    proj_ref,
    dtw_ref,
    bias_ref,
    rate_ref,
    skip_ref,
    states_ref,
    slot_ref,
    stream_ref,
    gain_ref,
    router_ref,
    routes_ref,
    out_hbm,
    gate_hbm,
    up_hbm,
    down_hbm,
    new_ref,
    mixed_ref,
    low_s,
    u_s,
    gin_s,
    step_s,
    drive_s,
    y_s,
    carried_s,
    obuf,
    gbuf,
    ubuf,
    dbuf,
    stage1,
    rs1,
    res_s,
    ag,
    xs,
    gacc,
    uacc,
    hid,
    stage2,
    rs2,
    osem,
    gsem,
    usem,
    dsem,
    send1,
    recv1,
    send2,
    recv2,
    send3,
    recv3,
):
    n_dp, n_e, n_t = sizes
    n_dev = n_dp * n_e * n_t
    n_blk = n_dp * n_e
    n_grp = n_e * n_t
    unroll = n_dev <= UNROLL_LIMIT
    dp = lax.axis_index("dp")
    ex = lax.axis_index("expert")
    te = lax.axis_index("tensor")
    rows, steps, chans = conv_ref.shape
    own_rows = stream_ref.shape[0]
    toks = own_rows * steps
    feat = mixed_ref.shape[2]
    width = stream_ref.shape[2]
    ff = gbuf.shape[2]
    all_toks = n_blk * toks
    blk = dp * n_e + ex
    grp = ex * n_t + te
    order = [lax.rem(te + k, n_t) for k in range(n_t)]

    def tensor_at(k):
        return lax.rem(te + k, n_t)

    barrier = pltpu.get_barrier_semaphore()

    def others(fn):
        if unroll:
            for c in range(n_t):
                for b in range(n_e):
                    for a in range(n_dp):
                        if a or b or c:
                            fn(lax.rem(dp + a, n_dp), lax.rem(ex + b, n_e), lax.rem(te + c, n_t))
        else:
            me = blk * n_t + te

            def body(j, carry):
                d = lax.rem(me + j, n_dev)
                fn(d // n_grp, lax.rem(d // n_t, n_e), lax.rem(d, n_t))
                return carry

            lax.fori_loop(1, n_dev, body, 0)

    def greet(a, b, c):
        pl.semaphore_signal(barrier, inc=1, device_id=(a, b, c), device_id_type=MESH)

    def o_copy(k):
        t = tensor_at(k)
        return pltpu.make_async_copy(
            out_hbm.at[:, pl.ds(pl.multiple_of(t * feat, feat), feat)], obuf.at[t], osem.at[k]
        )

    def g_copy(k):
        t = tensor_at(k)
        return pltpu.make_async_copy(
            gate_hbm.at[0, pl.ds(pl.multiple_of(t * feat, feat), feat), :], gbuf.at[t], gsem.at[k]
        )

    def u_copy(k):
        t = tensor_at(k)
        return pltpu.make_async_copy(
            up_hbm.at[0, pl.ds(pl.multiple_of(t * feat, feat), feat), :], ubuf.at[t], usem.at[k]
        )

    def d_copy(k):
        t = tensor_at(k)
        return pltpu.make_async_copy(
            down_hbm.at[0, :, pl.ds(pl.multiple_of(t * feat, feat), feat)], dbuf.at[t], dsem.at[k]
        )

    far_first = [(k + 1) % n_t for k in range(n_t)]
    for k in far_first:
        o_copy(k).start()
    others(greet)
    for k in range(n_t):
        g_copy(k).start()
        u_copy(k).start()
    for k in far_first:
        d_copy(k).start()

    for r in range(rows):
        low_s[steps * r : steps * (r + 1), :] = low_ref[r].astype(F32)
        u_s[steps * r : steps * (r + 1), :] = conv_ref[r].astype(F32)
        gin_s[steps * r : steps * (r + 1), :] = gate_in_ref[r].astype(F32)
    raw = jnp.dot(low_s[...].astype(BF16), dtw_ref[...], preferred_element_type=F32) + bias_ref[...]
    step_size = jnp.maximum(raw, 0.0) + jnp.log1p(jnp.exp(-jnp.abs(raw)))
    step_s[...] = step_size
    drive_s[...] = step_size * u_s[...]
    n_state = rate_ref.shape[0]
    eye = lax.broadcasted_iota(jnp.int32, (n_state, n_state), 0) == lax.broadcasted_iota(
        jnp.int32, (n_state, n_state), 1
    )
    rate = rate_ref[...]
    for r in range(rows):
        carried = states_ref[slot_ref[r]]
        for s in range(steps):
            i = steps * r + s
            b_col = jnp.sum(jnp.where(eye, proj_ref[r, s, 0:1, :], 0.0), axis=1, keepdims=True)
            c_col = jnp.sum(jnp.where(eye, proj_ref[r, s, 1:2, :], 0.0), axis=1, keepdims=True)
            decay = jnp.exp(-step_s[i : i + 1, :] * rate)
            carried = decay * carried + drive_s[i : i + 1, :] * b_col
            y_s[i : i + 1, :] = jnp.sum(c_col * carried, axis=0, keepdims=True)
        carried_s[r] = carried
    mixer_y = ((y_s[...] + skip_ref[...] * u_s[...]) * silu(gin_s[...])).astype(BF16)

    pl.semaphore_wait(barrier, n_dev - 1)

    tile_c = tile_of(feat)
    for k in far_first:
        t = tensor_at(k)
        o_copy(k).wait()
        for c in range(0, feat, tile_c):
            part = jnp.dot(mixer_y, obuf[t, :, c : c + tile_c], preferred_element_type=F32)
            for e in range(n_e):
                stage1[t * n_e + e, :, c : c + tile_c] = part[toks * e : toks * (e + 1)].astype(BF16)
        for b in range(n_e):
            if b == 0 and k == 0:
                continue
            e = lax.rem(ex + b, n_e)
            slot = lax.rem(e * n_t + t - grp + n_grp, n_grp) - 1
            pltpu.make_async_remote_copy(
                src_ref=stage1.at[t * n_e + e],
                dst_ref=rs1.at[slot],
                send_sem=send1,
                recv_sem=recv1,
                device_id=(dp, e, t),
                device_id_type=MESH,
            ).start()

    def slot_body(s, carry):
        value = states_ref[s]
        for r in range(rows):
            value = jnp.where(slot_ref[r] == s, carried_s[r], value)
        new_ref[s] = value
        return carry

    lax.fori_loop(0, states_ref.shape[0], slot_body, 0)

    own_cols = pl.ds(pl.multiple_of(te * feat, feat), feat)
    for i in range(own_rows):
        res_s[steps * i : steps * (i + 1), :] = stream_ref[i, :, own_cols].astype(F32)
    total = res_s[...] + stage1[te * n_e + ex].astype(F32)
    pltpu.make_async_copy(rs1, rs1, recv1).wait()
    for j in range(n_grp - 1):
        total = total + rs1[j].astype(F32)
    res_s[...] = total
    square = jnp.sum(total * total, axis=1, keepdims=True)
    high = square.astype(BF16).astype(F32)
    lane = lax.broadcasted_iota(jnp.int32, (toks, 128), 1)
    mine = te * n_blk + blk
    ag[mine, :, :feat] = (total * gain_ref[te]).astype(BF16)
    ag[mine, :, feat:] = jnp.where(lane < 64, high, square - high).astype(BF16)

    def spread(a, b, c):
        pltpu.make_async_remote_copy(
            src_ref=ag.at[mine],
            dst_ref=ag.at[mine],
            send_sem=send2,
            recv_sem=recv2.at[te],
            device_id=(a, b, c),
            device_id_type=MESH,
        ).start()

    others(spread)

    gacc[...] = jnp.zeros_like(gacc)
    uacc[...] = jnp.zeros_like(uacc)
    tile_f = tile_of(ff)

    def absorb(k, square_sum, logits):
        t = tensor_at(k)
        for b in range(n_blk):
            xs[toks * b : toks * (b + 1), :] = ag[t * n_blk + b].astype(F32)
        square_sum = square_sum + xs[:, feat : feat + 1] + xs[:, feat + 64 : feat + 65]
        own = ag[t * n_blk + blk, :, :feat].astype(F32)
        logits = [
            logits[e] + jnp.sum(own * router_ref[t, e : e + 1, :].astype(F32), axis=1, keepdims=True)
            for e in range(n_e)
        ]
        x = xs[:, :feat].astype(BF16)
        g_copy(k).wait()
        u_copy(k).wait()
        for c in range(0, ff, tile_f):
            gacc[:, c : c + tile_f] += jnp.dot(
                x, gbuf[t, :, c : c + tile_f], preferred_element_type=F32
            )
            uacc[:, c : c + tile_f] += jnp.dot(
                x, ubuf[t, :, c : c + tile_f], preferred_element_type=F32
            )
        return square_sum, logits

    square_sum = jnp.zeros((all_toks, 1), F32)
    logits = [jnp.zeros((toks, 1), F32) for _ in range(n_e)]
    for k in range(n_t):
        t = tensor_at(k)
        if k == 0:
            if n_blk > 1:
                piece = ag.at[pl.ds(0, n_blk - 1)]
                pltpu.make_async_copy(piece, piece, recv2.at[t]).wait()
        else:
            piece = ag.at[pl.ds(t * n_blk, n_blk)]
            pltpu.make_async_copy(piece, piece, recv2.at[t]).wait()
        square_sum, logits = absorb(k, square_sum, logits)
    scale = lax.rsqrt(square_sum / width + 1e-5)
    for c in range(0, ff, tile_f):
        g = gacc[:, c : c + tile_f] * scale
        hid[:, c : c + tile_f] = (silu(g) * (uacc[:, c : c + tile_f] * scale)).astype(BF16)

    for k in far_first:
        t = tensor_at(k)
        d_copy(k).wait()
        for c in range(0, feat, tile_c):
            part = jnp.dot(hid[...], dbuf[t, :, c : c + tile_c], preferred_element_type=F32)
            for b in range(n_blk):
                stage2[t * n_blk + b, :, c : c + tile_c] = part[toks * b : toks * (b + 1)].astype(BF16)
        place = ex * (n_dp * n_t) + dp * n_t + te

        def give(a, b):
            pltpu.make_async_remote_copy(
                src_ref=stage2.at[t * n_blk + a * n_e + b],
                dst_ref=rs2.at[place],
                send_sem=send3,
                recv_sem=recv3,
                device_id=(a, b, t),
                device_id_type=MESH,
            ).start()

        for a in range(n_dp):
            for b in range(n_e):
                if a == 0 and b == 0 and k == 0:
                    continue
                give(lax.rem(dp + a, n_dp), lax.rem(ex + b, n_e))

    own_square = jnp.zeros((toks, 1), F32)
    for t in range(n_t):
        tail = ag[t * n_blk + blk, :, feat:].astype(F32)
        own_square = own_square + tail[:, 0:1] + tail[:, 64:65]
    own_scale = lax.rsqrt(own_square / width + 1e-5)
    row = lax.broadcasted_iota(jnp.int32, (toks, 1), 0)
    first = jnp.zeros((toks, 1), jnp.int32)
    second = jnp.zeros((toks, 1), jnp.int32)
    for i in range(toks):
        first = jnp.where(row == i, routes_ref[i // steps, i % steps, 0], first)
        second = jnp.where(row == i, routes_ref[i // steps, i % steps, 1], second)
    margin = jnp.zeros((toks, 1), F32)
    for e in range(n_e):
        margin = margin + jnp.where(first == e, logits[e], 0.0) - jnp.where(second == e, logits[e], 0.0)
    weight_a = 1.0 / (1.0 + jnp.exp(-margin * own_scale))
    weight_b = 1.0 - weight_a
    coeffs = [
        jnp.where(first == e, weight_a, 0.0) + jnp.where(second == e, weight_b, 0.0)
        for e in range(n_e)
    ]
    total = res_s[...]
    rs2[ex * (n_dp * n_t) + dp * n_t + te] = stage2[te * n_blk + blk]
    gathered = rs2.at[pl.ds(0, n_dev - 1)]
    pltpu.make_async_copy(gathered, gathered, recv3).wait()
    for e in range(n_e):
        part = jnp.zeros((toks, feat), F32)
        for j in range(n_dp * n_t):
            part = part + rs2[e * n_dp * n_t + j].astype(F32)
        total = total + coeffs[e] * part
    for i in range(own_rows):
        mixed_ref[i] = total[steps * i : steps * (i + 1)].astype(BF16)

    pltpu.make_async_copy(rs1, rs1, send1).wait()
    sent = ag.at[pl.ds(0, n_dev - 1)]
    pltpu.make_async_copy(sent, sent, send2).wait()
    pltpu.make_async_copy(gathered, gathered, send3).wait()


def on_device(
    sizes,
    conv_out,
    gate_in,
    dt_low,
    state_proj,
    dt_weight,
    dt_bias,
    decay_rate,
    skip_gain,
    states,
    slot_ids,
    out_proj,
    stream,
    norm_gain,
    router,
    routes,
    gate_w,
    up_w,
    down_w,
):
    n_dp, n_e, n_t = sizes
    n_dev = n_dp * n_e * n_t
    n_blk = n_dp * n_e
    rows, steps, chans = conv_out.shape
    own_rows, _, width = stream.shape
    toks = own_rows * steps
    feat = width // n_t
    ff = gate_w.shape[2]
    all_toks = n_blk * toks
    vmem = pl.BlockSpec(memory_space=pltpu.VMEM)
    smem = pl.BlockSpec(memory_space=pltpu.SMEM)
    hbm = pl.BlockSpec(memory_space=pl.ANY)
    flat = rows * steps
    dma = pltpu.SemaphoreType.DMA
    return pl.pallas_call(
        functools.partial(kernel, sizes),
        out_shape=(
            jax.ShapeDtypeStruct(states.shape, F32),
            jax.ShapeDtypeStruct((own_rows, steps, feat), BF16),
        ),
        in_specs=[vmem] * 9 + [smem] + [vmem] * 3 + [smem] + [hbm] * 4,
        out_specs=(vmem, vmem),
        scratch_shapes=[
            pltpu.VMEM((flat, dt_low.shape[2]), F32),
            pltpu.VMEM((flat, chans), F32),
            pltpu.VMEM((flat, chans), F32),
            pltpu.VMEM((flat, chans), F32),
            pltpu.VMEM((flat, chans), F32),
            pltpu.VMEM((flat, chans), F32),
            pltpu.VMEM((rows,) + states.shape[1:], F32),
            pltpu.VMEM((n_t, chans, feat), BF16),
            pltpu.VMEM((n_t, feat, ff), BF16),
            pltpu.VMEM((n_t, feat, ff), BF16),
            pltpu.VMEM((n_t, ff, feat), BF16),
            pltpu.VMEM((n_t * n_e, toks, feat), BF16),
            pltpu.VMEM((n_t * n_e - 1, toks, feat), BF16),
            pltpu.VMEM((toks, feat), F32),
            pltpu.VMEM((n_dev, toks, feat + 128), BF16),
            pltpu.VMEM((all_toks, feat + 128), F32),
            pltpu.VMEM((all_toks, ff), F32),
            pltpu.VMEM((all_toks, ff), F32),
            pltpu.VMEM((all_toks, ff), BF16),
            pltpu.VMEM((n_dev, toks, feat), BF16),
            pltpu.VMEM((n_dev, toks, feat), BF16),
            dma((n_t,)),
            dma((n_t,)),
            dma((n_t,)),
            dma((n_t,)),
            dma,
            dma,
            dma,
            dma((n_t,)),
            dma,
            dma,
        ],
        compiler_params=pltpu.CompilerParams(
            collective_id=0, has_side_effects=True, vmem_limit_bytes=60 * 1024 * 1024
        ),
    )(
        conv_out,
        gate_in,
        dt_low,
        state_proj,
        dt_weight,
        dt_bias.reshape(1, -1),
        decay_rate,
        skip_gain.reshape(1, -1),
        states,
        slot_ids,
        stream,
        norm_gain.reshape(n_t, 1, feat),
        router.T.reshape(-1, n_t, feat).transpose(1, 0, 2),
        routes,
        out_proj,
        gate_w,
        up_w,
        down_w,
    )


def solution(mesh):
    sizes = (mesh.shape["dp"], mesh.shape["expert"], mesh.shape["tensor"])
    return jax.shard_map(
        functools.partial(on_device, sizes),
        mesh=mesh,
        in_specs=(
            P("dp", None, ("expert", "tensor")),
            P("dp", None, ("expert", "tensor")),
            P("dp", None, None),
            P("dp", None, None, None),
            P(None, ("expert", "tensor")),
            P(("expert", "tensor")),
            P(None, ("expert", "tensor")),
            P(("expert", "tensor")),
            P("dp", None, ("expert", "tensor")),
            P("dp"),
            P(("expert", "tensor"), None),
            P(("dp", "expert"), None, None),
            P(),
            P(),
            P(("dp", "expert"), None, None),
            P("expert", None, ("dp", "tensor")),
            P("expert", None, ("dp", "tensor")),
            P("expert", ("dp", "tensor"), None),
        ),
        out_specs=(P("dp", None, ("expert", "tensor")), P(("dp", "expert"), None, "tensor")),
        check_vma=False,
    )
```

```python
import functools

import jax
import jax.numpy as jnp
from jax import lax
from jax.experimental import pallas as pl
from jax.experimental.pallas import tpu as pltpu
from jax.sharding import PartitionSpec as P

MESH = pl.DeviceIdType.MESH
UNROLL_LIMIT = 8
F32 = jnp.float32
BF16 = jnp.bfloat16


def tile_of(extent):
    return 512 if extent % 512 == 0 else extent


def silu(v):
    return v / (1.0 + jnp.exp(-v))


def nearest_first(position, count):
    places = []
    for k in range(count):
        value = 0
        for p in range(count):
            ranked = sorted(range(count), key=lambda q: (abs(q - p), q))
            value = jnp.where(position == p, ranked[k], value)
        places.append(value)
    return places


def kernel(
    sizes,
    conv_ref,
    gate_in_ref,
    low_ref,
    proj_ref,
    dtw_ref,
    bias_ref,
    rate_ref,
    skip_ref,
    states_ref,
    slot_ref,
    stream_ref,
    gain_ref,
    router_ref,
    routes_ref,
    out_hbm,
    gate_hbm,
    up_hbm,
    down_hbm,
    new_ref,
    mixed_ref,
    low_s,
    u_s,
    gin_s,
    step_s,
    drive_s,
    y_s,
    carried_s,
    obuf,
    gbuf,
    ubuf,
    dbuf,
    stage1,
    rs1,
    res_s,
    ag,
    xs,
    gacc,
    uacc,
    hid,
    stage2,
    plane_in,
    stage3,
    along_in,
    osem,
    gsem,
    usem,
    dsem,
    send1,
    recv1,
    send2,
    along2,
    recv2,
    send3,
    recv3,
    send4,
    recv4,
):
    n_dp, n_e, n_t = sizes
    n_dev = n_dp * n_e * n_t
    n_blk = n_dp * n_e
    n_grp = n_e * n_t
    unroll = n_blk <= UNROLL_LIMIT
    dp = lax.axis_index("dp")
    ex = lax.axis_index("expert")
    te = lax.axis_index("tensor")
    rows, steps, chans = conv_ref.shape
    own_rows = stream_ref.shape[0]
    toks = own_rows * steps
    feat = mixed_ref.shape[2]
    width = stream_ref.shape[2]
    ff = gbuf.shape[2]
    all_toks = n_blk * toks
    blk = dp * n_e + ex
    grp = ex * n_t + te
    near = nearest_first(te, n_t)

    def tensor_at(k):
        return near[k]

    def plane(fn):
        if unroll:
            for a in range(n_dp):
                for b in range(n_e):
                    if a or b:
                        fn(lax.rem(dp + a, n_dp), lax.rem(ex + b, n_e))
        else:

            def body(j, carry):
                q = lax.rem(blk + j, n_blk)
                fn(q // n_e, lax.rem(q, n_e))
                return carry

            lax.fori_loop(1, n_blk, body, 0)

    barrier = pltpu.get_barrier_semaphore()

    def greet(a, b, c):
        pl.semaphore_signal(barrier, inc=1, device_id=(a, b, c), device_id_type=MESH)

    def greet_all():
        for c in range(1, n_t):
            for b in range(n_e):
                greet(dp, lax.rem(ex + b, n_e), lax.rem(te + c, n_t))
        plane(lambda a, b: greet(a, b, te))

    def o_copy(k):
        t = tensor_at(k)
        return pltpu.make_async_copy(
            out_hbm.at[:, pl.ds(pl.multiple_of(t * feat, feat), feat)], obuf.at[t], osem.at[k]
        )

    def g_copy(k):
        t = tensor_at(k)
        return pltpu.make_async_copy(
            gate_hbm.at[0, pl.ds(pl.multiple_of(t * feat, feat), feat), :], gbuf.at[t], gsem.at[k]
        )

    def u_copy(k):
        t = tensor_at(k)
        return pltpu.make_async_copy(
            up_hbm.at[0, pl.ds(pl.multiple_of(t * feat, feat), feat), :], ubuf.at[t], usem.at[k]
        )

    def d_copy(k):
        t = tensor_at(k)
        return pltpu.make_async_copy(
            down_hbm.at[0, :, pl.ds(pl.multiple_of(t * feat, feat), feat)], dbuf.at[t], dsem.at[k]
        )

    far_first = list(reversed(range(n_t)))
    for k in far_first:
        o_copy(k).start()
    greet_all()
    for k in range(n_t):
        g_copy(k).start()
        u_copy(k).start()
    for k in far_first:
        d_copy(k).start()

    for r in range(rows):
        low_s[steps * r : steps * (r + 1), :] = low_ref[r].astype(F32)
        u_s[steps * r : steps * (r + 1), :] = conv_ref[r].astype(F32)
        gin_s[steps * r : steps * (r + 1), :] = gate_in_ref[r].astype(F32)
    raw = jnp.dot(low_s[...].astype(BF16), dtw_ref[...], preferred_element_type=F32) + bias_ref[...]
    step_size = jnp.maximum(raw, 0.0) + jnp.log1p(jnp.exp(-jnp.abs(raw)))
    step_s[...] = step_size
    drive_s[...] = step_size * u_s[...]
    n_state = rate_ref.shape[0]
    eye = lax.broadcasted_iota(jnp.int32, (n_state, n_state), 0) == lax.broadcasted_iota(
        jnp.int32, (n_state, n_state), 1
    )
    rate = rate_ref[...]
    for r in range(rows):
        carried = states_ref[slot_ref[r]]
        for s in range(steps):
            i = steps * r + s
            b_col = jnp.sum(jnp.where(eye, proj_ref[r, s, 0:1, :], 0.0), axis=1, keepdims=True)
            c_col = jnp.sum(jnp.where(eye, proj_ref[r, s, 1:2, :], 0.0), axis=1, keepdims=True)
            decay = jnp.exp(-step_s[i : i + 1, :] * rate)
            carried = decay * carried + drive_s[i : i + 1, :] * b_col
            y_s[i : i + 1, :] = jnp.sum(c_col * carried, axis=0, keepdims=True)
        carried_s[r] = carried
    mixer_y = ((y_s[...] + skip_ref[...] * u_s[...]) * silu(gin_s[...])).astype(BF16)

    pl.semaphore_wait(barrier, (n_t - 1) * n_e + n_blk - 1)

    tile_c = tile_of(feat)
    for k in far_first:
        t = tensor_at(k)
        o_copy(k).wait()
        for c in range(0, feat, tile_c):
            part = jnp.dot(mixer_y, obuf[t, :, c : c + tile_c], preferred_element_type=F32)
            for e in range(n_e):
                stage1[t * n_e + e, :, c : c + tile_c] = part[toks * e : toks * (e + 1)].astype(BF16)
        for b in range(n_e):
            if b == 0 and k == 0:
                continue
            e = lax.rem(ex + b, n_e)
            slot = lax.rem(e * n_t + t - grp + n_grp, n_grp) - 1
            pltpu.make_async_remote_copy(
                src_ref=stage1.at[t * n_e + e],
                dst_ref=rs1.at[slot],
                send_sem=send1,
                recv_sem=recv1,
                device_id=(dp, e, t),
                device_id_type=MESH,
            ).start()

    def slot_body(s, carry):
        value = states_ref[s]
        for r in range(rows):
            value = jnp.where(slot_ref[r] == s, carried_s[r], value)
        new_ref[s] = value
        return carry

    lax.fori_loop(0, states_ref.shape[0], slot_body, 0)

    own_cols = pl.ds(pl.multiple_of(te * feat, feat), feat)
    for i in range(own_rows):
        res_s[steps * i : steps * (i + 1), :] = stream_ref[i, :, own_cols].astype(F32)
    total = res_s[...] + stage1[te * n_e + ex].astype(F32)
    pltpu.make_async_copy(rs1, rs1, recv1).wait()
    for j in range(n_grp - 1):
        total = total + rs1[j].astype(F32)
    res_s[...] = total
    square = jnp.sum(total * total, axis=1, keepdims=True)
    high = square.astype(BF16).astype(F32)
    lane = lax.broadcasted_iota(jnp.int32, (toks, 128), 1)
    mine = te * n_blk + blk
    ag[mine, :, :feat] = (total * gain_ref[te]).astype(BF16)
    ag[mine, :, feat:] = jnp.where(lane < 64, high, square - high).astype(BF16)

    for k in far_first[:-1]:
        pltpu.make_async_remote_copy(
            src_ref=ag.at[mine],
            dst_ref=ag.at[mine],
            send_sem=send2,
            recv_sem=along2.at[te],
            device_id=(dp, ex, tensor_at(k)),
            device_id_type=MESH,
        ).start()

    def relay(k):
        t = tensor_at(k)
        piece = ag.at[t * n_blk + blk]
        if k:
            pltpu.make_async_copy(piece, piece, along2.at[t]).wait()

        def spread(a, b):
            pltpu.make_async_remote_copy(
                src_ref=piece,
                dst_ref=piece,
                send_sem=send2,
                recv_sem=recv2.at[t],
                device_id=(a, b, te),
                device_id_type=MESH,
            ).start()

        plane(spread)

    for k in range(max(n_t - 1, 1)):
        relay(k)

    gacc[...] = jnp.zeros_like(gacc)
    uacc[...] = jnp.zeros_like(uacc)
    tile_f = tile_of(ff)

    def absorb(k, square_sum, logits):
        t = tensor_at(k)
        for b in range(n_blk):
            xs[toks * b : toks * (b + 1), :] = ag[t * n_blk + b].astype(F32)
        square_sum = square_sum + xs[:, feat : feat + 1] + xs[:, feat + 64 : feat + 65]
        own = ag[t * n_blk + blk, :, :feat].astype(F32)
        logits = [
            logits[e] + jnp.sum(own * router_ref[t, e : e + 1, :].astype(F32), axis=1, keepdims=True)
            for e in range(n_e)
        ]
        x = xs[:, :feat].astype(BF16)
        g_copy(k).wait()
        u_copy(k).wait()
        for c in range(0, ff, tile_f):
            gacc[:, c : c + tile_f] += jnp.dot(
                x, gbuf[t, :, c : c + tile_f], preferred_element_type=F32
            )
            uacc[:, c : c + tile_f] += jnp.dot(
                x, ubuf[t, :, c : c + tile_f], preferred_element_type=F32
            )
        return square_sum, logits

    square_sum = jnp.zeros((all_toks, 1), F32)
    logits = [jnp.zeros((toks, 1), F32) for _ in range(n_e)]
    for k in range(n_t):
        if n_blk > 1:
            piece = ag.at[pl.ds(0, n_blk - 1)]
            pltpu.make_async_copy(piece, piece, recv2.at[tensor_at(k)]).wait()
        square_sum, logits = absorb(k, square_sum, logits)
        if k == 0 and n_t > 1:
            relay(n_t - 1)
    scale = lax.rsqrt(square_sum / width + 1e-5)
    for c in range(0, ff, tile_f):
        g = gacc[:, c : c + tile_f] * scale
        hid[:, c : c + tile_f] = (silu(g) * (uacc[:, c : c + tile_f] * scale)).astype(BF16)

    for k in far_first:
        t = tensor_at(k)
        d_copy(k).wait()
        for c in range(0, feat, tile_c):
            part = jnp.dot(hid[...], dbuf[t, :, c : c + tile_c], preferred_element_type=F32)
            for b in range(n_blk):
                stage2[t * n_blk + b, :, c : c + tile_c] = part[toks * b : toks * (b + 1)].astype(BF16)

        def give(a, b):
            pltpu.make_async_remote_copy(
                src_ref=stage2.at[t * n_blk + a * n_e + b],
                dst_ref=plane_in.at[t * n_blk + blk],
                send_sem=send3,
                recv_sem=recv3.at[t],
                device_id=(a, b, te),
                device_id_type=MESH,
            ).start()

        plane(give)

    own_square = jnp.zeros((toks, 1), F32)
    for t in range(n_t):
        tail = ag[t * n_blk + blk, :, feat:].astype(F32)
        own_square = own_square + tail[:, 0:1] + tail[:, 64:65]
    own_scale = lax.rsqrt(own_square / width + 1e-5)
    row = lax.broadcasted_iota(jnp.int32, (toks, 1), 0)
    first = jnp.zeros((toks, 1), jnp.int32)
    second = jnp.zeros((toks, 1), jnp.int32)
    for i in range(toks):
        first = jnp.where(row == i, routes_ref[i // steps, i % steps, 0], first)
        second = jnp.where(row == i, routes_ref[i // steps, i % steps, 1], second)
    margin = jnp.zeros((toks, 1), F32)
    for e in range(n_e):
        margin = margin + jnp.where(first == e, logits[e], 0.0) - jnp.where(second == e, logits[e], 0.0)
    weight_a = 1.0 / (1.0 + jnp.exp(-margin * own_scale))
    weight_b = 1.0 - weight_a
    coeffs = [
        jnp.where(first == e, weight_a, 0.0) + jnp.where(second == e, weight_b, 0.0)
        for e in range(n_e)
    ]
    for k in far_first:
        t = tensor_at(k)
        if n_blk > 1:
            piece = plane_in.at[pl.ds(0, n_blk - 1)]
            pltpu.make_async_copy(piece, piece, recv3.at[t]).wait()
        plane_in[t * n_blk + blk] = stage2[t * n_blk + blk]
        total = jnp.zeros((toks, feat), F32)
        for e in range(n_e):
            part = jnp.zeros((toks, feat), F32)
            for a in range(n_dp):
                part = part + plane_in[t * n_blk + a * n_e + e].astype(F32)
            total = total + coeffs[e] * part
        if k:
            stage3[k - 1] = total.astype(BF16)
            slot = lax.rem(te - t + n_t, n_t) - 1
            pltpu.make_async_remote_copy(
                src_ref=stage3.at[k - 1],
                dst_ref=along_in.at[slot],
                send_sem=send4,
                recv_sem=recv4,
                device_id=(dp, ex, t),
                device_id_type=MESH,
            ).start()
    total = total + res_s[...]
    if n_t > 1:
        pltpu.make_async_copy(along_in, along_in, recv4).wait()
        for j in range(n_t - 1):
            total = total + along_in[j].astype(F32)
    for i in range(own_rows):
        mixed_ref[i] = total[steps * i : steps * (i + 1)].astype(BF16)

    pltpu.make_async_copy(rs1, rs1, send1).wait()
    sent = ag.at[pl.ds(0, n_dev - 1)]
    pltpu.make_async_copy(sent, sent, send2).wait()
    given = stage2.at[pl.ds(0, (n_blk - 1) * n_t)]
    pltpu.make_async_copy(given, given, send3).wait()
    if n_t > 1:
        pltpu.make_async_copy(stage3, stage3, send4).wait()


def on_device(
    sizes,
    conv_out,
    gate_in,
    dt_low,
    state_proj,
    dt_weight,
    dt_bias,
    decay_rate,
    skip_gain,
    states,
    slot_ids,
    out_proj,
    stream,
    norm_gain,
    router,
    routes,
    gate_w,
    up_w,
    down_w,
):
    n_dp, n_e, n_t = sizes
    n_dev = n_dp * n_e * n_t
    n_blk = n_dp * n_e
    rows, steps, chans = conv_out.shape
    own_rows, _, width = stream.shape
    toks = own_rows * steps
    feat = width // n_t
    ff = gate_w.shape[2]
    all_toks = n_blk * toks
    vmem = pl.BlockSpec(memory_space=pltpu.VMEM)
    smem = pl.BlockSpec(memory_space=pltpu.SMEM)
    hbm = pl.BlockSpec(memory_space=pl.ANY)
    flat = rows * steps
    dma = pltpu.SemaphoreType.DMA
    return pl.pallas_call(
        functools.partial(kernel, sizes),
        out_shape=(
            jax.ShapeDtypeStruct(states.shape, F32),
            jax.ShapeDtypeStruct((own_rows, steps, feat), BF16),
        ),
        in_specs=[vmem] * 9 + [smem] + [vmem] * 3 + [smem] + [hbm] * 4,
        out_specs=(vmem, vmem),
        scratch_shapes=[
            pltpu.VMEM((flat, dt_low.shape[2]), F32),
            pltpu.VMEM((flat, chans), F32),
            pltpu.VMEM((flat, chans), F32),
            pltpu.VMEM((flat, chans), F32),
            pltpu.VMEM((flat, chans), F32),
            pltpu.VMEM((flat, chans), F32),
            pltpu.VMEM((rows,) + states.shape[1:], F32),
            pltpu.VMEM((n_t, chans, feat), BF16),
            pltpu.VMEM((n_t, feat, ff), BF16),
            pltpu.VMEM((n_t, feat, ff), BF16),
            pltpu.VMEM((n_t, ff, feat), BF16),
            pltpu.VMEM((n_t * n_e, toks, feat), BF16),
            pltpu.VMEM((n_t * n_e - 1, toks, feat), BF16),
            pltpu.VMEM((toks, feat), F32),
            pltpu.VMEM((n_dev, toks, feat + 128), BF16),
            pltpu.VMEM((all_toks, feat + 128), F32),
            pltpu.VMEM((all_toks, ff), F32),
            pltpu.VMEM((all_toks, ff), F32),
            pltpu.VMEM((all_toks, ff), BF16),
            pltpu.VMEM((n_dev, toks, feat), BF16),
            pltpu.VMEM((n_dev, toks, feat), BF16),
            pltpu.VMEM((max(n_t - 1, 1), toks, feat), BF16),
            pltpu.VMEM((max(n_t - 1, 1), toks, feat), BF16),
            dma((n_t,)),
            dma((n_t,)),
            dma((n_t,)),
            dma((n_t,)),
            dma,
            dma,
            dma,
            dma((n_t,)),
            dma((n_t,)),
            dma,
            dma((n_t,)),
            dma,
            dma,
        ],
        compiler_params=pltpu.CompilerParams(
            collective_id=0, has_side_effects=True, vmem_limit_bytes=60 * 1024 * 1024
        ),
    )(
        conv_out,
        gate_in,
        dt_low,
        state_proj,
        dt_weight,
        dt_bias.reshape(1, -1),
        decay_rate,
        skip_gain.reshape(1, -1),
        states,
        slot_ids,
        stream,
        norm_gain.reshape(n_t, 1, feat),
        router.T.reshape(-1, n_t, feat).transpose(1, 0, 2),
        routes,
        out_proj,
        gate_w,
        up_w,
        down_w,
    )


def solution(mesh):
    sizes = (mesh.shape["dp"], mesh.shape["expert"], mesh.shape["tensor"])
    return jax.shard_map(
        functools.partial(on_device, sizes),
        mesh=mesh,
        in_specs=(
            P("dp", None, ("expert", "tensor")),
            P("dp", None, ("expert", "tensor")),
            P("dp", None, None),
            P("dp", None, None, None),
            P(None, ("expert", "tensor")),
            P(("expert", "tensor")),
            P(None, ("expert", "tensor")),
            P(("expert", "tensor")),
            P("dp", None, ("expert", "tensor")),
            P("dp"),
            P(("expert", "tensor"), None),
            P(("dp", "expert"), None, None),
            P(),
            P(),
            P(("dp", "expert"), None, None),
            P("expert", None, ("dp", "tensor")),
            P("expert", None, ("dp", "tensor")),
            P("expert", ("dp", "tensor"), None),
        ),
        out_specs=(P("dp", None, ("expert", "tensor")), P(("dp", "expert"), None, "tensor")),
        check_vma=False,
    )
```

```python
import functools

import jax
import jax.numpy as jnp
from jax import lax
from jax.experimental import pallas as pl
from jax.experimental.pallas import tpu as pltpu
from jax.sharding import PartitionSpec as P

MESH = pl.DeviceIdType.MESH
UNROLL_LIMIT = 8
F32 = jnp.float32
BF16 = jnp.bfloat16


def tile_of(extent):
    return 512 if extent % 512 == 0 else extent


def silu(v):
    return v / (1.0 + jnp.exp(-v))


def nearest_first(position, count):
    places = []
    for k in range(count):
        value = 0
        for p in range(count):
            ranked = sorted(range(count), key=lambda q: (abs(q - p), q))
            value = jnp.where(position == p, ranked[k], value)
        places.append(value)
    return places


def kernel(
    sizes,
    conv_hbm,
    gate_in_hbm,
    low_hbm,
    proj_hbm,
    dtw_hbm,
    bias_hbm,
    rate_hbm,
    skip_hbm,
    states_hbm,
    slot_hbm,
    stream_hbm,
    gain_hbm,
    router_hbm,
    routes_hbm,
    out_hbm,
    gate_hbm,
    up_hbm,
    down_hbm,
    new_hbm,
    mixed_ref,
    conv_ref,
    gate_in_ref,
    low_ref,
    proj_ref,
    dtw_ref,
    bias_ref,
    rate_ref,
    skip_ref,
    states_ref,
    slot_ref,
    stream_ref,
    gain_ref,
    router_ref,
    routes_ref,
    new_ref,
    in_sem,
    new_sem,
    low_s,
    u_s,
    gin_s,
    step_s,
    drive_s,
    y_s,
    carried_s,
    obuf,
    gbuf,
    ubuf,
    dbuf,
    stage1,
    rs1,
    res_s,
    ag,
    xs,
    gacc,
    uacc,
    hid,
    stage2,
    plane_in,
    stage3,
    along_in,
    osem,
    gsem,
    usem,
    dsem,
    send1,
    recv1,
    send2,
    along2,
    recv2,
    send3,
    recv3,
    send4,
    recv4,
):
    n_dp, n_e, n_t = sizes
    n_dev = n_dp * n_e * n_t
    n_blk = n_dp * n_e
    n_grp = n_e * n_t
    unroll = n_blk <= UNROLL_LIMIT
    dp = lax.axis_index("dp")
    ex = lax.axis_index("expert")
    te = lax.axis_index("tensor")
    rows, steps, chans = conv_ref.shape
    own_rows = stream_ref.shape[0]
    toks = own_rows * steps
    feat = mixed_ref.shape[2]
    width = stream_ref.shape[2]
    ff = gbuf.shape[2]
    all_toks = n_blk * toks
    blk = dp * n_e + ex
    grp = ex * n_t + te
    near = nearest_first(te, n_t)

    def tensor_at(k):
        return near[k]

    def plane(fn):
        if unroll:
            for a in range(n_dp):
                for b in range(n_e):
                    if a or b:
                        fn(lax.rem(dp + a, n_dp), lax.rem(ex + b, n_e))
        else:

            def body(j, carry):
                q = lax.rem(blk + j, n_blk)
                fn(q // n_e, lax.rem(q, n_e))
                return carry

            lax.fori_loop(1, n_blk, body, 0)

    barrier = pltpu.get_barrier_semaphore()

    def greet(a, b, c):
        pl.semaphore_signal(barrier, inc=1, device_id=(a, b, c), device_id_type=MESH)

    def greet_all():
        for c in range(1, n_t):
            for b in range(n_e):
                greet(dp, lax.rem(ex + b, n_e), lax.rem(te + c, n_t))
        plane(lambda a, b: greet(a, b, te))

    def o_copy(k):
        t = tensor_at(k)
        return pltpu.make_async_copy(
            out_hbm.at[:, pl.ds(pl.multiple_of(t * feat, feat), feat)], obuf.at[t], osem.at[k]
        )

    def g_copy(k):
        t = tensor_at(k)
        return pltpu.make_async_copy(
            gate_hbm.at[0, pl.ds(pl.multiple_of(t * feat, feat), feat), :], gbuf.at[t], gsem.at[k]
        )

    def u_copy(k):
        t = tensor_at(k)
        return pltpu.make_async_copy(
            up_hbm.at[0, pl.ds(pl.multiple_of(t * feat, feat), feat), :], ubuf.at[t], usem.at[k]
        )

    def d_copy(k):
        t = tensor_at(k)
        return pltpu.make_async_copy(
            down_hbm.at[0, :, pl.ds(pl.multiple_of(t * feat, feat), feat)], dbuf.at[t], dsem.at[k]
        )

    far_first = list(reversed(range(n_t)))
    greet_all()
    loads = [
        pltpu.make_async_copy(source, target, in_sem.at[j])
        for j, (source, target) in enumerate(
            (
                (low_hbm, low_ref),
                (dtw_hbm, dtw_ref),
                (bias_hbm, bias_ref),
                (conv_hbm, conv_ref),
                (gate_in_hbm, gate_in_ref),
                (proj_hbm, proj_ref),
                (rate_hbm, rate_ref),
                (skip_hbm, skip_ref),
                (slot_hbm, slot_ref),
                (states_hbm, states_ref),
                (stream_hbm, stream_ref),
                (gain_hbm, gain_ref),
                (router_hbm, router_ref),
                (routes_hbm, routes_ref),
            )
        )
    ]
    for load in loads:
        load.start()
    for k in far_first:
        o_copy(k).start()

    for load in loads:
        load.wait()
    for r in range(rows):
        low_s[steps * r : steps * (r + 1), :] = low_ref[r].astype(F32)
        u_s[steps * r : steps * (r + 1), :] = conv_ref[r].astype(F32)
        gin_s[steps * r : steps * (r + 1), :] = gate_in_ref[r].astype(F32)
    raw = jnp.dot(low_s[...].astype(BF16), dtw_ref[...], preferred_element_type=F32) + bias_ref[...]
    step_size = jnp.maximum(raw, 0.0) + jnp.log1p(jnp.exp(-jnp.abs(raw)))
    step_s[...] = step_size
    drive_s[...] = step_size * u_s[...]
    n_state = rate_ref.shape[0]
    eye = lax.broadcasted_iota(jnp.int32, (n_state, n_state), 0) == lax.broadcasted_iota(
        jnp.int32, (n_state, n_state), 1
    )
    rate = rate_ref[...]
    for r in range(rows):
        carried = states_ref[slot_ref[r]]
        for s in range(steps):
            i = steps * r + s
            b_col = jnp.sum(jnp.where(eye, proj_ref[r, s, 0:1, :], 0.0), axis=1, keepdims=True)
            c_col = jnp.sum(jnp.where(eye, proj_ref[r, s, 1:2, :], 0.0), axis=1, keepdims=True)
            decay = jnp.exp(-step_s[i : i + 1, :] * rate)
            carried = decay * carried + drive_s[i : i + 1, :] * b_col
            y_s[i : i + 1, :] = jnp.sum(c_col * carried, axis=0, keepdims=True)
        carried_s[r] = carried
    mixer_y = ((y_s[...] + skip_ref[...] * u_s[...]) * silu(gin_s[...])).astype(BF16)

    for k in range(n_t):
        g_copy(k).start()
        u_copy(k).start()
    for k in far_first:
        d_copy(k).start()
    pl.semaphore_wait(barrier, (n_t - 1) * n_e + n_blk - 1)

    tile_c = tile_of(feat)
    for k in far_first:
        t = tensor_at(k)
        o_copy(k).wait()
        for c in range(0, feat, tile_c):
            part = jnp.dot(mixer_y, obuf[t, :, c : c + tile_c], preferred_element_type=F32)
            for e in range(n_e):
                stage1[t * n_e + e, :, c : c + tile_c] = part[toks * e : toks * (e + 1)].astype(BF16)
        for b in range(n_e):
            if b == 0 and k == 0:
                continue
            e = lax.rem(ex + b, n_e)
            slot = lax.rem(e * n_t + t - grp + n_grp, n_grp) - 1
            pltpu.make_async_remote_copy(
                src_ref=stage1.at[t * n_e + e],
                dst_ref=rs1.at[slot],
                send_sem=send1,
                recv_sem=recv1,
                device_id=(dp, e, t),
                device_id_type=MESH,
            ).start()

    def slot_body(s, carry):
        value = states_ref[s]
        for r in range(rows):
            value = jnp.where(slot_ref[r] == s, carried_s[r], value)
        new_ref[s] = value
        return carry

    lax.fori_loop(0, states_ref.shape[0], slot_body, 0)

    pltpu.make_async_copy(new_ref, new_hbm, new_sem).start()
    own_cols = pl.ds(pl.multiple_of(te * feat, feat), feat)
    for i in range(own_rows):
        res_s[steps * i : steps * (i + 1), :] = stream_ref[i, :, own_cols].astype(F32)
    total = res_s[...] + stage1[te * n_e + ex].astype(F32)
    pltpu.make_async_copy(rs1, rs1, recv1).wait()
    for j in range(n_grp - 1):
        total = total + rs1[j].astype(F32)
    res_s[...] = total
    square = jnp.sum(total * total, axis=1, keepdims=True)
    high = square.astype(BF16).astype(F32)
    lane = lax.broadcasted_iota(jnp.int32, (toks, 128), 1)
    mine = te * n_blk + blk
    ag[mine, :, :feat] = (total * gain_ref[te]).astype(BF16)
    ag[mine, :, feat:] = jnp.where(lane < 64, high, square - high).astype(BF16)

    for k in far_first[:-1]:
        pltpu.make_async_remote_copy(
            src_ref=ag.at[mine],
            dst_ref=ag.at[mine],
            send_sem=send2,
            recv_sem=along2.at[te],
            device_id=(dp, ex, tensor_at(k)),
            device_id_type=MESH,
        ).start()

    def relay(k):
        t = tensor_at(k)
        piece = ag.at[t * n_blk + blk]
        if k:
            pltpu.make_async_copy(piece, piece, along2.at[t]).wait()

        def spread(a, b):
            pltpu.make_async_remote_copy(
                src_ref=piece,
                dst_ref=piece,
                send_sem=send2,
                recv_sem=recv2.at[t],
                device_id=(a, b, te),
                device_id_type=MESH,
            ).start()

        plane(spread)

    for k in range(max(n_t - 1, 1)):
        relay(k)

    gacc[...] = jnp.zeros_like(gacc)
    uacc[...] = jnp.zeros_like(uacc)
    tile_f = tile_of(ff)

    def absorb(k, square_sum, logits):
        t = tensor_at(k)
        for b in range(n_blk):
            xs[toks * b : toks * (b + 1), :] = ag[t * n_blk + b].astype(F32)
        square_sum = square_sum + xs[:, feat : feat + 1] + xs[:, feat + 64 : feat + 65]
        own = ag[t * n_blk + blk, :, :feat].astype(F32)
        logits = [
            logits[e] + jnp.sum(own * router_ref[t, e : e + 1, :].astype(F32), axis=1, keepdims=True)
            for e in range(n_e)
        ]
        x = xs[:, :feat].astype(BF16)
        g_copy(k).wait()
        u_copy(k).wait()
        for c in range(0, ff, tile_f):
            gacc[:, c : c + tile_f] += jnp.dot(
                x, gbuf[t, :, c : c + tile_f], preferred_element_type=F32
            )
            uacc[:, c : c + tile_f] += jnp.dot(
                x, ubuf[t, :, c : c + tile_f], preferred_element_type=F32
            )
        return square_sum, logits

    square_sum = jnp.zeros((all_toks, 1), F32)
    logits = [jnp.zeros((toks, 1), F32) for _ in range(n_e)]
    for k in range(n_t):
        if n_blk > 1:
            piece = ag.at[pl.ds(0, n_blk - 1)]
            pltpu.make_async_copy(piece, piece, recv2.at[tensor_at(k)]).wait()
        square_sum, logits = absorb(k, square_sum, logits)
        if k == 0 and n_t > 1:
            relay(n_t - 1)
    scale = lax.rsqrt(square_sum / width + 1e-5)
    for c in range(0, ff, tile_f):
        g = gacc[:, c : c + tile_f] * scale
        hid[:, c : c + tile_f] = (silu(g) * (uacc[:, c : c + tile_f] * scale)).astype(BF16)

    for k in far_first:
        t = tensor_at(k)
        d_copy(k).wait()
        for c in range(0, feat, tile_c):
            part = jnp.dot(hid[...], dbuf[t, :, c : c + tile_c], preferred_element_type=F32)
            for b in range(n_blk):
                stage2[t * n_blk + b, :, c : c + tile_c] = part[toks * b : toks * (b + 1)].astype(BF16)

        def give(a, b):
            pltpu.make_async_remote_copy(
                src_ref=stage2.at[t * n_blk + a * n_e + b],
                dst_ref=plane_in.at[t * n_blk + blk],
                send_sem=send3,
                recv_sem=recv3.at[t],
                device_id=(a, b, te),
                device_id_type=MESH,
            ).start()

        plane(give)

    own_square = jnp.zeros((toks, 1), F32)
    for t in range(n_t):
        tail = ag[t * n_blk + blk, :, feat:].astype(F32)
        own_square = own_square + tail[:, 0:1] + tail[:, 64:65]
    own_scale = lax.rsqrt(own_square / width + 1e-5)
    row = lax.broadcasted_iota(jnp.int32, (toks, 1), 0)
    first = jnp.zeros((toks, 1), jnp.int32)
    second = jnp.zeros((toks, 1), jnp.int32)
    for i in range(toks):
        first = jnp.where(row == i, routes_ref[i // steps, i % steps, 0], first)
        second = jnp.where(row == i, routes_ref[i // steps, i % steps, 1], second)
    margin = jnp.zeros((toks, 1), F32)
    for e in range(n_e):
        margin = margin + jnp.where(first == e, logits[e], 0.0) - jnp.where(second == e, logits[e], 0.0)
    weight_a = 1.0 / (1.0 + jnp.exp(-margin * own_scale))
    weight_b = 1.0 - weight_a
    coeffs = [
        jnp.where(first == e, weight_a, 0.0) + jnp.where(second == e, weight_b, 0.0)
        for e in range(n_e)
    ]
    for k in far_first:
        t = tensor_at(k)
        if n_blk > 1:
            piece = plane_in.at[pl.ds(0, n_blk - 1)]
            pltpu.make_async_copy(piece, piece, recv3.at[t]).wait()
        plane_in[t * n_blk + blk] = stage2[t * n_blk + blk]
        total = jnp.zeros((toks, feat), F32)
        for e in range(n_e):
            part = jnp.zeros((toks, feat), F32)
            for a in range(n_dp):
                part = part + plane_in[t * n_blk + a * n_e + e].astype(F32)
            total = total + coeffs[e] * part
        if k:
            stage3[k - 1] = total.astype(BF16)
            slot = lax.rem(te - t + n_t, n_t) - 1
            pltpu.make_async_remote_copy(
                src_ref=stage3.at[k - 1],
                dst_ref=along_in.at[slot],
                send_sem=send4,
                recv_sem=recv4,
                device_id=(dp, ex, t),
                device_id_type=MESH,
            ).start()
    total = total + res_s[...]
    if n_t > 1:
        pltpu.make_async_copy(along_in, along_in, recv4).wait()
        for j in range(n_t - 1):
            total = total + along_in[j].astype(F32)
    for i in range(own_rows):
        mixed_ref[i] = total[steps * i : steps * (i + 1)].astype(BF16)

    pltpu.make_async_copy(new_ref, new_hbm, new_sem).wait()
    pltpu.make_async_copy(rs1, rs1, send1).wait()
    sent = ag.at[pl.ds(0, n_dev - 1)]
    pltpu.make_async_copy(sent, sent, send2).wait()
    given = stage2.at[pl.ds(0, (n_blk - 1) * n_t)]
    pltpu.make_async_copy(given, given, send3).wait()
    if n_t > 1:
        pltpu.make_async_copy(stage3, stage3, send4).wait()


def finish(new_in, mixed_in, new_out, mixed_out, new_s, mixed_s, in_sem, out_sem):
    parts = in_sem.shape[0] - 1
    size = new_in.shape[0] // parts
    into = [pltpu.make_async_copy(mixed_in, mixed_s, in_sem.at[parts])]
    out = [pltpu.make_async_copy(mixed_s, mixed_out, out_sem.at[parts])]
    for j in range(parts):
        piece = pl.ds(j * size, size)
        into.append(pltpu.make_async_copy(new_in.at[piece], new_s.at[piece], in_sem.at[j]))
        out.append(pltpu.make_async_copy(new_s.at[piece], new_out.at[piece], out_sem.at[j]))
    for copy in into:
        copy.start()
    for arrive, leave in zip(into, out):
        arrive.wait()
        leave.start()
    for copy in out:
        copy.wait()


def on_device(
    sizes,
    conv_out,
    gate_in,
    dt_low,
    state_proj,
    dt_weight,
    dt_bias,
    decay_rate,
    skip_gain,
    states,
    slot_ids,
    out_proj,
    stream,
    norm_gain,
    router,
    routes,
    gate_w,
    up_w,
    down_w,
):
    n_dp, n_e, n_t = sizes
    n_dev = n_dp * n_e * n_t
    n_blk = n_dp * n_e
    rows, steps, chans = conv_out.shape
    own_rows, _, width = stream.shape
    toks = own_rows * steps
    feat = width // n_t
    ff = gate_w.shape[2]
    all_toks = n_blk * toks
    vmem = pl.BlockSpec(memory_space=pltpu.VMEM)
    hbm = pl.BlockSpec(memory_space=pl.ANY)
    flat = rows * steps
    dma = pltpu.SemaphoreType.DMA
    small = (
        conv_out,
        gate_in,
        dt_low,
        state_proj,
        dt_weight,
        dt_bias.reshape(1, -1),
        decay_rate,
        skip_gain.reshape(1, -1),
        states,
        slot_ids,
        stream,
        norm_gain.reshape(n_t, 1, feat),
        router.T.reshape(-1, n_t, feat).transpose(1, 0, 2),
        routes,
    )
    in_smem = (9, 13)
    new_states, mixed = pl.pallas_call(
        functools.partial(kernel, sizes),
        out_shape=(
            jax.ShapeDtypeStruct(states.shape, F32),
            jax.ShapeDtypeStruct((own_rows, steps, feat), BF16),
        ),
        in_specs=[hbm] * 18,
        out_specs=(hbm, vmem),
        scratch_shapes=[
            (pltpu.SMEM if j in in_smem else pltpu.VMEM)(value.shape, value.dtype)
            for j, value in enumerate(small)
        ]
        + [
            pltpu.VMEM(states.shape, F32),
            dma((len(small),)),
            dma,
            pltpu.VMEM((flat, dt_low.shape[2]), F32),
            pltpu.VMEM((flat, chans), F32),
            pltpu.VMEM((flat, chans), F32),
            pltpu.VMEM((flat, chans), F32),
            pltpu.VMEM((flat, chans), F32),
            pltpu.VMEM((flat, chans), F32),
            pltpu.VMEM((rows,) + states.shape[1:], F32),
            pltpu.VMEM((n_t, chans, feat), BF16),
            pltpu.VMEM((n_t, feat, ff), BF16),
            pltpu.VMEM((n_t, feat, ff), BF16),
            pltpu.VMEM((n_t, ff, feat), BF16),
            pltpu.VMEM((n_t * n_e, toks, feat), BF16),
            pltpu.VMEM((n_t * n_e - 1, toks, feat), BF16),
            pltpu.VMEM((toks, feat), F32),
            pltpu.VMEM((n_dev, toks, feat + 128), BF16),
            pltpu.VMEM((all_toks, feat + 128), F32),
            pltpu.VMEM((all_toks, ff), F32),
            pltpu.VMEM((all_toks, ff), F32),
            pltpu.VMEM((all_toks, ff), BF16),
            pltpu.VMEM((n_dev, toks, feat), BF16),
            pltpu.VMEM((n_dev, toks, feat), BF16),
            pltpu.VMEM((max(n_t - 1, 1), toks, feat), BF16),
            pltpu.VMEM((max(n_t - 1, 1), toks, feat), BF16),
            dma((n_t,)),
            dma((n_t,)),
            dma((n_t,)),
            dma((n_t,)),
            dma,
            dma,
            dma,
            dma((n_t,)),
            dma((n_t,)),
            dma,
            dma((n_t,)),
            dma,
            dma,
        ],
        compiler_params=pltpu.CompilerParams(
            collective_id=0, has_side_effects=True, vmem_limit_bytes=60 * 1024 * 1024
        ),
    )(
        *small,
        out_proj,
        gate_w,
        up_w,
        down_w,
    )
    return pl.pallas_call(
        finish,
        out_shape=(
            jax.ShapeDtypeStruct(states.shape, F32),
            jax.ShapeDtypeStruct((own_rows, steps, feat), BF16),
        ),
        in_specs=[hbm, hbm],
        out_specs=(hbm, hbm),
        scratch_shapes=[
            pltpu.VMEM(states.shape, F32),
            pltpu.VMEM((own_rows, steps, feat), BF16),
            dma((5 if states.shape[0] % 4 == 0 else 2,)),
            dma((5 if states.shape[0] % 4 == 0 else 2,)),
        ],
    )(new_states, mixed)


def solution(mesh):
    sizes = (mesh.shape["dp"], mesh.shape["expert"], mesh.shape["tensor"])
    return jax.shard_map(
        functools.partial(on_device, sizes),
        mesh=mesh,
        in_specs=(
            P("dp", None, ("expert", "tensor")),
            P("dp", None, ("expert", "tensor")),
            P("dp", None, None),
            P("dp", None, None, None),
            P(None, ("expert", "tensor")),
            P(("expert", "tensor")),
            P(None, ("expert", "tensor")),
            P(("expert", "tensor")),
            P("dp", None, ("expert", "tensor")),
            P("dp"),
            P(("expert", "tensor"), None),
            P(("dp", "expert"), None, None),
            P(),
            P(),
            P(("dp", "expert"), None, None),
            P("expert", None, ("dp", "tensor")),
            P("expert", None, ("dp", "tensor")),
            P("expert", ("dp", "tensor"), None),
        ),
        out_specs=(P("dp", None, ("expert", "tensor")), P(("dp", "expert"), None, "tensor")),
        check_vma=False,
    )
```
